32 devices in a mesh: depth: 8 (over y, x, core), tile: 4 (over z).
Axes of the slice: x: 2, y: 2, z: 4, core: 2. Of those that a mesh axis runs over, the one named last changes fastest.
Arguments:
- field: float32 [32, 384, 1024], P('depth', 'tile'), may hold values from -6 to 6
Outputs:
- image: float32 [4, 384, 1024], P(None, ('tile', 'depth'))
The draws below stay inside these ranges and needn't reach their ends.
All inputs are finite; a program needn't handle non-finite values.
Results may differ from the reference program's by a relative error of at most 0.0003.
Values sent between devices are 32-bit elements; how exact they have to be, the bound alone decides.
A program may use at most 64 MiB of HBM per device.

```python
import jax
import jax.numpy as jnp
from jax import lax

ROWS = 96
COLS = 1024
NZ = 32
HEIGHT = 384
N_TILE = 4


def level_of(key, extent, shards, least, high):
    gain, own = 1.0, jax.random.fold_in(key, 6)
    for position, shards_of in shards:
        steps = jnp.exp(jax.random.uniform(jax.random.fold_in(own, position), (shards_of,), jnp.float32, least / len(shards), high / len(shards)))
        gain = gain * jnp.repeat(steps, extent[position] // shards_of).reshape([-1 if axis == position else 1 for axis in range(len(extent))])
    return gain


def centred(rng, extent, width, limit, pieces=(), held_as=jnp.bfloat16):
    level = level_of(rng, extent, pieces, -0.22, 0.18) if pieces else 1.0
    result = jax.random.normal(rng, extent, jnp.float32) * width * level
    return jnp.minimum(jnp.maximum(result, -limit), limit).astype(held_as)


def setup_inputs(seed: int = 0) -> dict:
    key_of = jax.random.split(jax.random.key(seed), 2)
    field = centred(key_of[0], (NZ, HEIGHT, COLS), 1.0, 6.0, ((0, 8), (1, 4)), jnp.float32)
    return {"field": field}


centres = (-1.2, 0.3, 1.5)
spreads = (0.25, 0.35, 0.3)
heights = (2.0, 1.0, 3.0)
floor_density = 0.05
light_cols = 0.48
light_rows = 0.6
light_depth = 0.64

def emission(sample, slope_cols, slope_rows, slope_depth):
    density = floor_density + jnp.zeros_like(sample)
    for centre, spread, bump_height in zip(centres, spreads, heights):
        scaled = (sample - centre) / spread
        density = density + bump_height * jnp.exp(-scaled * scaled)
    facing = light_cols * slope_cols + light_rows * slope_rows + light_depth * slope_depth
    length = slope_cols * slope_cols + slope_rows * slope_rows + slope_depth * slope_depth + 1.0
    shading = 0.3 + 0.7 * jnp.abs(facing) * lax.rsqrt(length)
    colour = jnp.stack([shading * jax.nn.sigmoid(2.0 * sample), shading * jnp.exp(-sample * sample), shading * jax.nn.sigmoid(-2.0 * sample)])
    return (density, colour)

def integrate(density, colour, spacing):
    optics = spacing * density
    running = jnp.cumsum(optics, axis=0)
    before = jnp.concatenate([jnp.zeros_like(optics[:1]), running[:-1]], axis=0)
    weight = jnp.exp(-before) * -jnp.expm1(-optics)
    return (lax.optimization_barrier(jnp.sum(weight[None] * colour, axis=1)), jnp.exp(-running[-1]))

def reference(field):
    spacing = 3.0 / NZ
    height = field.shape[1]

    def one_block(block_index):
        first_row = block_index * ROWS
        has_below = (first_row > 0).astype(field.dtype)
        has_above = (first_row + ROWS < height).astype(field.dtype)
        row_below = lax.dynamic_slice_in_dim(field, jnp.maximum(first_row - 1, 0).astype(jnp.int32), 1, 1) * has_below
        middle = lax.dynamic_slice_in_dim(field, first_row.astype(jnp.int32), ROWS, 1)
        higher = lax.dynamic_slice_in_dim(field, jnp.minimum(first_row + ROWS, height - 1).astype(jnp.int32), 1, 1) * has_above
        window = jnp.concatenate([row_below, middle, higher], axis=1)
        further = jnp.concatenate([window[1:], jnp.zeros_like(window[:1])], axis=0)
        sample = 0.5 * (window + further)
        slope_depth = (further - window)[:, 1:-1]
        slope_rows = 0.5 * (sample[:, 2:] - sample[:, :-2])
        sample = sample[:, 1:-1]
        zero_col = jnp.zeros_like(sample[..., :1])
        slope_cols = 0.5 * (jnp.concatenate([sample[..., 1:], zero_col], axis=-1) - jnp.concatenate([zero_col, sample[..., :-1]], axis=-1))
        density, colour = emission(sample, slope_cols, slope_rows, slope_depth)
        colour_sum, through = integrate(density, colour, spacing)
        return jnp.concatenate([colour_sum, (1.0 - through)[None]], axis=0)
    blocks = lax.map(one_block, jnp.arange(N_TILE, dtype=jnp.int32))
    return jnp.transpose(blocks, (1, 0, 2, 3)).reshape(4, N_TILE * ROWS, field.shape[2])
```

```python
import functools
import math

import jax
import jax.numpy as jnp
from jax import lax
from jax.experimental import pallas as pl
from jax.experimental.pallas import tpu as pltpu
from jax.sharding import PartitionSpec as P

centres = (-1.2, 0.3, 1.5)
spreads = (0.25, 0.35, 0.3)
heights = (2.0, 1.0, 3.0)
floor_density = 0.05
light_cols = 0.48
light_rows = 0.6
light_depth = 0.64

LOG2E = math.log2(math.e)
SUB, LANE = 8, 128


def kernel(
    dims, field, out, raw, behind, grid, low_send, high_send, low, high,
    parts, pair, send, pieces, result,
    raw_sem, plane_sem, edge_send_sem, edge_recv_sem, pair_send_sem, pair_recv_sem,
    piece_send_sem, piece_recv_sem,
):
    planes, rows, cols, depth_count, tile_count = dims
    chips = depth_count // 2
    share = rows // depth_count
    spacing = 3.0 / (planes * depth_count)
    group = max(g for g in range(1, 5) if share % g == 0)
    me = lax.axis_index("depth")
    tile = lax.axis_index("tile")
    chip = me // 2
    core = me % 2
    partner = chip * 2 + (1 - core)

    def remote(src, dst, send_sem, recv_sem, depth_to, tile_to):
        return pltpu.make_async_remote_copy(
            src_ref=src, dst_ref=dst, send_sem=send_sem, recv_sem=recv_sem,
            device_id=(depth_to, tile_to), device_id_type=pl.DeviceIdType.MESH,
        )

    loads = [pltpu.make_async_copy(field.at[p], raw.at[p], raw_sem.at[p]) for p in range(planes)]
    for load in loads:
        load.start()

    has_front = me > 0
    has_behind = me < depth_count - 1
    has_low = tile > 0
    has_high = tile < tile_count - 1
    near = [
        (has_front, me - 1, tile),
        (has_behind, me + 1, tile),
        (has_low, me, tile - 1),
        (has_high, me, tile + 1),
        (has_front & has_low, me - 1, tile - 1),
        (has_front & has_high, me - 1, tile + 1),
        (has_behind & has_low, me + 1, tile - 1),
        (has_behind & has_high, me + 1, tile + 1),
    ]
    barrier = pltpu.get_barrier_semaphore()
    for cond, d, t in near:
        @pl.when(cond)
        def _(d=d, t=t):
            pl.semaphore_signal(barrier, inc=1, device_id=(d, t), device_id_type=pl.DeviceIdType.MESH)
    pl.semaphore_signal(barrier, inc=1, device_id=(partner, tile), device_id_type=pl.DeviceIdType.MESH)
    for step in range(chips - 1):
        other = (chip + step + 1) % chips * 2 + core
        pl.semaphore_signal(barrier, inc=1, device_id=(other, tile), device_id_type=pl.DeviceIdType.MESH)
    greeted = chips
    for cond, _, _ in near:
        greeted = greeted + cond.astype(jnp.int32)
    pl.semaphore_wait(barrier, greeted)

    front = remote(field.at[0], behind, plane_sem.at[0], plane_sem.at[1], me - 1, tile)

    @pl.when(has_front)
    def _():
        front.start()

    def spread(source, p):
        for r in range(0, rows, SUB):
            for j in range(cols // LANE):
                grid[p, pl.ds((r + 1) * SUB + j, SUB, stride=SUB), :] = source[
                    r : r + SUB, j * LANE : (j + 1) * LANE
                ]

    first, last = pl.ds(SUB, SUB), pl.ds(rows * SUB, SUB)
    for p in range(planes):
        loads[p].wait()
        spread(raw.at[p], p)
        low_send[p] = grid[p, first, :]
        high_send[p] = grid[p, last, :]
    own = pl.ds(0, planes)
    to_low = remote(low_send, high.at[own], edge_send_sem.at[0], edge_recv_sem.at[0], me, tile - 1)
    to_high = remote(high_send, low.at[own], edge_send_sem.at[1], edge_recv_sem.at[1], me, tile + 1)
    corner_low = remote(
        low_send.at[0], high.at[planes], edge_send_sem.at[2], edge_recv_sem.at[2], me - 1, tile - 1
    )
    corner_high = remote(
        high_send.at[0], low.at[planes], edge_send_sem.at[3], edge_recv_sem.at[3], me - 1, tile + 1
    )
    sends = [
        (has_low, to_low),
        (has_high, to_high),
        (has_front & has_low, corner_low),
        (has_front & has_high, corner_high),
    ]
    for cond, copy in sends:
        @pl.when(cond)
        def _(copy=copy):
            copy.start()

    below, above = pl.ds(0, SUB), pl.ds((rows + 1) * SUB, SUB)
    blank = jnp.zeros((SUB, LANE), jnp.float32)

    def fill(cond, copy, where, halo, which):
        @pl.when(cond)
        def _():
            copy.wait_recv()
            for p in which:
                grid[p, where, :] = halo[p]

        @pl.when(jnp.logical_not(cond))
        def _():
            for p in which:
                grid[p, where, :] = blank

    fill(has_high, to_low, above, high, range(planes))
    fill(has_low, to_high, below, low, range(planes))

    lane = lax.broadcasted_iota(jnp.int32, (group, SUB, LANE), 2)
    sub = lax.broadcasted_iota(jnp.int32, (group, SUB, LANE), 1)
    left_edge = lane == 0
    right_edge = lane == LANE - 1
    left_end = left_edge & (sub == 0)
    right_end = right_edge & (sub == SUB - 1)
    scale = spacing * LOG2E

    def plane_step(p, row, state):
        red, blue, green, through = state
        at = pl.ds(pl.multiple_of(row * SUB, SUB), (group + 2) * SUB)
        here = grid[p, at, :].reshape(group + 2, SUB, LANE)
        there = grid[p + 1, at, :].reshape(group + 2, SUB, LANE)
        total = here + there
        twice = total[1:-1]
        d_depth = there[1:-1] - here[1:-1]
        d_rows = total[2:] - total[:-2]
        from_left = pltpu.roll(twice, 1, 2)
        from_left = jnp.where(left_edge, pltpu.roll(from_left, 1, 1), from_left)
        from_left = jnp.where(left_end, 0.0, from_left)
        from_right = pltpu.roll(twice, LANE - 1, 2)
        from_right = jnp.where(right_edge, pltpu.roll(from_right, SUB - 1, 1), from_right)
        from_right = jnp.where(right_end, 0.0, from_right)
        d_cols = from_right - from_left
        facing = (0.25 * light_cols) * d_cols + (0.25 * light_rows) * d_rows + light_depth * d_depth
        length = (d_cols * d_cols + d_rows * d_rows) * 0.0625 + (d_depth * d_depth + 1.0)
        shading = 0.3 + 0.7 * jnp.abs(facing) * lax.rsqrt(length)
        optics = scale * floor_density
        for centre, width, bump in zip(centres, spreads, heights):
            root = math.sqrt(LOG2E) / width
            scaled = (0.5 * root) * twice - root * centre
            optics = optics + jnp.exp2(math.log2(bump * scale) - scaled * scaled)
        after = through * jnp.exp2(-optics)
        lit = (through - after) * shading
        middle = jnp.exp2((twice * (-0.25 * LOG2E)) * twice)
        balance = jnp.tanh(0.5 * twice)
        return (red + lit, blue + lit * balance, green + lit * middle, after)

    width = share * SUB

    def put(chunk, offset, state):
        at = pl.ds(pl.multiple_of(offset * SUB, SUB), group * SUB)
        for c in range(4):
            parts[chunk, c, at, :] = state[c].reshape(group * SUB, LANE)

    zero = jnp.zeros((group, SUB, LANE), jnp.float32)
    per_share = share // group

    def early(i, carry):
        state = (zero, zero, zero, zero + 1.0)
        for p in range(planes - 1):
            state = plane_step(p, i * group, state)
        put(i // per_share, i % per_share * group, state)
        return carry

    lax.fori_loop(0, rows // group, early, 0)

    @pl.when(has_behind)
    def _():
        front.wait_recv()
        spread(behind, planes)

    @pl.when(jnp.logical_not(has_behind))
    def _():
        grid[planes] = jnp.zeros(grid.shape[1:], jnp.float32)

    fill(has_behind & has_high, corner_low, above, high, (planes,))
    fill(has_behind & has_low, corner_high, below, low, (planes,))

    def late(chunk):
        def body(i, carry):
            at = pl.ds(pl.multiple_of(i * group * SUB, SUB), group * SUB)
            state = tuple(parts[chunk, c, at, :].reshape(group, SUB, LANE) for c in range(4))
            put(chunk, i * group, plane_step(planes - 1, chunk * share + i * group, state))
            return carry

        lax.fori_loop(0, per_share, body, 0)

    order = [(chip + step + 1) % chips for step in range(chips)]
    pair_copies = []
    for step, q in enumerate(order):
        chunk = q * 2 + (1 - core)
        late(chunk)
        copy = remote(parts.at[chunk], pair.at[step], pair_send_sem.at[step], pair_recv_sem.at[step], partner, tile)
        copy.start()
        pair_copies.append(copy)

    in_front = core == 0
    piece_copies = []
    for step, q in enumerate(order):
        chunk = q * 2 + core
        late(chunk)
        pair_copies[step].wait_recv()
        mine = [parts[chunk, c] for c in range(4)]
        theirs = [pair[step, c] for c in range(4)]
        near_through = jnp.where(in_front, mine[3], theirs[3])
        final = step == chips - 1
        target = pieces.at[chip] if final else send.at[step]
        for c in range(3):
            target[c] = jnp.where(in_front, mine[c], theirs[c]) + near_through * jnp.where(in_front, theirs[c], mine[c])
        target[3] = mine[3] * theirs[3]
        if not final:
            copy = remote(
                send.at[step], pieces.at[chip], piece_send_sem.at[step], piece_recv_sem.at[step],
                q * 2 + core, tile,
            )
            copy.start()
            piece_copies.append(copy)

    for copy in piece_copies:
        copy.wait_recv()
    colour = [pieces[0, c] for c in range(3)]
    through = pieces[0, 3]
    for k in range(1, chips):
        colour = [colour[c] + through * pieces[k, c] for c in range(3)]
        through = through * pieces[k, 3]
    result[0] = 0.5 * (colour[0] + colour[1])
    result[1] = colour[2]
    result[2] = 0.5 * (colour[0] - colour[1])
    result[3] = 1.0 - through
    for c in range(4):
        for j in range(cols // LANE):
            out[c, :, j * LANE : (j + 1) * LANE] = result[c, pl.ds(j, share, stride=SUB), :]

    for copy in pair_copies + piece_copies:
        copy.wait_send()
    for cond, copy in sends + [(has_front, front)]:
        @pl.when(cond)
        def _(copy=copy):
            copy.wait_send()


def local(field):
    planes, rows, cols = field.shape
    depth_count = lax.axis_size("depth")
    chips = depth_count // 2
    share = rows // depth_count
    f32 = jnp.float32
    dims = (planes, rows, cols, depth_count, lax.axis_size("tile"))
    dma = pltpu.SemaphoreType.DMA
    return pl.pallas_call(
        functools.partial(kernel, dims),
        out_shape=jax.ShapeDtypeStruct((4, share, cols), f32),
        in_specs=[pl.BlockSpec(memory_space=pl.ANY)],
        out_specs=pl.BlockSpec(memory_space=pltpu.VMEM),
        scratch_shapes=[
            pltpu.VMEM((planes, rows, cols), f32),
            pltpu.VMEM((rows, cols), f32),
            pltpu.VMEM((planes + 1, (rows + 2) * SUB, LANE), f32),
            pltpu.VMEM((planes, SUB, LANE), f32),
            pltpu.VMEM((planes, SUB, LANE), f32),
            pltpu.VMEM((planes + 1, SUB, LANE), f32),
            pltpu.VMEM((planes + 1, SUB, LANE), f32),
            pltpu.VMEM((depth_count, 4, share * SUB, LANE), f32),
            pltpu.VMEM((chips, 4, share * SUB, LANE), f32),
            pltpu.VMEM((chips, 4, share * SUB, LANE), f32),
            pltpu.VMEM((chips, 4, share * SUB, LANE), f32),
            pltpu.VMEM((4, share * SUB, LANE), f32),
            dma((planes,)),
            dma((2,)),
            dma((4,)),
            dma((4,)),
            dma((chips,)),
            dma((chips,)),
            dma((chips,)),
            dma((chips,)),
        ],
        compiler_params=pltpu.CompilerParams(collective_id=0, has_side_effects=True),
    )(field)


def solution(mesh):
    return jax.shard_map(
        local,
        mesh=mesh,
        in_specs=(P("depth", "tile", None),),
        out_specs=P(None, ("tile", "depth"), None),
        check_vma=False,
    )
```

```python
import functools
import math

import jax
import jax.numpy as jnp
from jax import lax
from jax.experimental import pallas as pl
from jax.experimental.pallas import tpu as pltpu
from jax.sharding import PartitionSpec as P

centres = (-1.2, 0.3, 1.5)
spreads = (0.25, 0.35, 0.3)
heights = (2.0, 1.0, 3.0)
floor_density = 0.05
light_cols = 0.48
light_rows = 0.6
light_depth = 0.64

LOG2E = math.log2(math.e)
SUB, LANE = 8, 128


def kernel(
    dims, field, out, raw, behind, grid, low_send, high_send, low, high,
    parts, pair, send, pieces, result,
    raw_sem, plane_send_sem, plane_recv_sem, edge_send_sem, edge_recv_sem, pair_send_sem, pair_recv_sem,
    piece_send_sem, piece_recv_sem,
):
    planes, rows, cols, depth_count, tile_count = dims
    chips = depth_count // 2
    share = rows // depth_count
    spacing = 3.0 / (planes * depth_count)
    group = max(g for g in range(1, 5) if share % g == 0)
    me = lax.axis_index("depth")
    tile = lax.axis_index("tile")
    chip = me // 2
    core = me % 2
    partner = chip * 2 + (1 - core)

    def remote(src, dst, send_sem, recv_sem, depth_to, tile_to):
        return pltpu.make_async_remote_copy(
            src_ref=src, dst_ref=dst, send_sem=send_sem, recv_sem=recv_sem,
            device_id=(depth_to, tile_to), device_id_type=pl.DeviceIdType.MESH,
        )

    loads = [pltpu.make_async_copy(field.at[p], raw.at[p], raw_sem.at[p]) for p in range(planes)]
    for load in loads:
        load.start()

    has_front = me > 0
    has_behind = me < depth_count - 1
    has_low = tile > 0
    has_high = tile < tile_count - 1
    near = [
        (has_front, me - 1, tile),
        (has_behind, me + 1, tile),
        (has_low, me, tile - 1),
        (has_high, me, tile + 1),
        (has_front & has_low, me - 1, tile - 1),
        (has_front & has_high, me - 1, tile + 1),
        (has_behind & has_low, me + 1, tile - 1),
        (has_behind & has_high, me + 1, tile + 1),
    ]
    barrier = pltpu.get_barrier_semaphore()
    for cond, d, t in near:
        @pl.when(cond)
        def _(d=d, t=t):
            pl.semaphore_signal(barrier, inc=1, device_id=(d, t), device_id_type=pl.DeviceIdType.MESH)
    pl.semaphore_signal(barrier, inc=1, device_id=(partner, tile), device_id_type=pl.DeviceIdType.MESH)
    for step in range(chips - 1):
        other = (chip + step + 1) % chips * 2 + core
        pl.semaphore_signal(barrier, inc=1, device_id=(other, tile), device_id_type=pl.DeviceIdType.MESH)
    def spread(source, p):
        for r in range(0, rows, SUB):
            for j in range(cols // LANE):
                grid[p, pl.ds((r + 1) * SUB + j, SUB, stride=SUB), :] = source[
                    r : r + SUB, j * LANE : (j + 1) * LANE
                ]

    first, last = pl.ds(SUB, SUB), pl.ds(rows * SUB, SUB)
    for p in range(planes):
        loads[p].wait()
        spread(raw.at[p], p)
        low_send[p] = grid[p, first, :]
        high_send[p] = grid[p, last, :]

    greeted = chips
    for cond, _, _ in near:
        greeted = greeted + cond.astype(jnp.int32)
    pl.semaphore_wait(barrier, greeted)

    block = 2 * share
    sends = []

    def plane_row(row, count):
        return grid.at[0, pl.ds(pl.multiple_of((row + 1) * SUB, SUB), count * SUB), :]

    strips = []
    for step in range(chips):
        q = ((me + depth_count - 1) // 2 + step + 1) % chips
        strip = []
        for k, (cond, row, count, place) in enumerate((
            (has_front, q * block, block, 1),
            (has_front & (q > 0), jnp.maximum(q * block - 1, 0), 1, 0),
            (has_front & (q < chips - 1), jnp.minimum((q + 1) * block, rows - 1), 1, block + 1),
        )):
            copy = remote(
                plane_row(row, count), behind.at[step, pl.ds(place * SUB, count * SUB), :],
                plane_send_sem.at[step, k], plane_recv_sem.at[step, k], me - 1, tile,
            )
            sends.append((cond, copy))
            strip.append(copy)
        strips.append(strip)
    own = pl.ds(0, planes)
    to_low = remote(low_send, high.at[own], edge_send_sem.at[0], edge_recv_sem.at[0], me, tile - 1)
    to_high = remote(high_send, low.at[own], edge_send_sem.at[1], edge_recv_sem.at[1], me, tile + 1)
    corner_low = remote(
        low_send.at[0], high.at[planes], edge_send_sem.at[2], edge_recv_sem.at[2], me - 1, tile - 1
    )
    corner_high = remote(
        high_send.at[0], low.at[planes], edge_send_sem.at[3], edge_recv_sem.at[3], me - 1, tile + 1
    )
    edges = [
        (has_low, to_low),
        (has_high, to_high),
        (has_front & has_low, corner_low),
        (has_front & has_high, corner_high),
    ]
    for cond, copy in edges + sends:
        @pl.when(cond)
        def _(copy=copy):
            copy.start()

    below, above = pl.ds(0, SUB), pl.ds((rows + 1) * SUB, SUB)
    blank = jnp.zeros((SUB, LANE), jnp.float32)

    def fill(cond, copy, where, halo, which):
        @pl.when(cond)
        def _():
            copy.wait_recv()
            for p in which:
                grid[p, where, :] = halo[p]

        @pl.when(jnp.logical_not(cond))
        def _():
            for p in which:
                grid[p, where, :] = blank

    fill(has_high, to_low, above, high, range(planes))
    fill(has_low, to_high, below, low, range(planes))

    lane = lax.broadcasted_iota(jnp.int32, (group, SUB, LANE), 2)
    sub = lax.broadcasted_iota(jnp.int32, (group, SUB, LANE), 1)
    left_edge = lane == 0
    right_edge = lane == LANE - 1
    left_end = left_edge & (sub == 0)
    right_end = right_edge & (sub == SUB - 1)
    scale = spacing * LOG2E

    def plane_step(p, row, state, there):
        red, blue, green, through = state
        at = pl.ds(pl.multiple_of(row * SUB, SUB), (group + 2) * SUB)
        here = grid[p, at, :].reshape(group + 2, SUB, LANE)
        there = there.reshape(group + 2, SUB, LANE)
        total = here + there
        twice = total[1:-1]
        d_depth = there[1:-1] - here[1:-1]
        d_rows = total[2:] - total[:-2]
        from_left = pltpu.roll(twice, 1, 2)
        from_left = jnp.where(left_edge, pltpu.roll(from_left, 1, 1), from_left)
        from_left = jnp.where(left_end, 0.0, from_left)
        from_right = pltpu.roll(twice, LANE - 1, 2)
        from_right = jnp.where(right_edge, pltpu.roll(from_right, SUB - 1, 1), from_right)
        from_right = jnp.where(right_end, 0.0, from_right)
        d_cols = from_right - from_left
        facing = (0.25 * light_cols) * d_cols + (0.25 * light_rows) * d_rows + light_depth * d_depth
        length = (d_cols * d_cols + d_rows * d_rows) * 0.0625 + (d_depth * d_depth + 1.0)
        shading = 0.3 + 0.7 * jnp.abs(facing) * lax.rsqrt(length)
        optics = scale * floor_density
        for centre, width, bump in zip(centres, spreads, heights):
            root = math.sqrt(LOG2E) / width
            scaled = (0.5 * root) * twice - root * centre
            optics = optics + jnp.exp2(math.log2(bump * scale) - scaled * scaled)
        after = through * jnp.exp2(-optics)
        lit = (through - after) * shading
        middle = jnp.exp2((twice * (-0.25 * LOG2E)) * twice)
        balance = jnp.tanh(0.5 * twice)
        return (red + lit, blue + lit * balance, green + lit * middle, after)

    width = share * SUB

    def put(chunk, offset, state):
        at = pl.ds(pl.multiple_of(offset * SUB, SUB), group * SUB)
        for c in range(4):
            parts[chunk, c, at, :] = state[c].reshape(group * SUB, LANE)

    zero = jnp.zeros((group, SUB, LANE), jnp.float32)
    per_share = share // group

    def window(row):
        return pl.ds(pl.multiple_of(row * SUB, SUB), (group + 2) * SUB)

    order = [(chip + step + 1) % chips for step in range(chips)]

    def early(step):
        q = order[step]

        def body(i, carry):
            state = (zero, zero, zero, zero + 1.0)
            row = q * block + i * group
            for p in range(planes - 1):
                state = plane_step(p, row, state, grid[p + 1, window(row), :])
            put(q * 2 + i // per_share, i % per_share * group, state)
            return carry

        lax.fori_loop(0, block // group, body, 0)

    def end(step, cond, have, copy, halo, place):
        at = pl.ds(place * SUB, SUB)

        @pl.when(cond & have)
        def _():
            copy.wait_recv()
            behind[step, at, :] = halo[planes]

        @pl.when(cond & jnp.logical_not(have))
        def _():
            behind[step, at, :] = blank

    def arrive(step):
        q = order[step]
        whole, lower, upper = strips[step]

        @pl.when(has_behind)
        def _():
            whole.wait_recv()

        @pl.when(has_behind & (q > 0))
        def _():
            lower.wait_recv()

        @pl.when(has_behind & (q < chips - 1))
        def _():
            upper.wait_recv()

        end(step, has_behind & (q == 0), has_low, corner_high, low, 0)
        end(step, has_behind & (q == chips - 1), has_high, corner_low, high, block + 1)

        @pl.when(jnp.logical_not(has_behind))
        def _():
            behind[step] = jnp.zeros(behind.shape[1:], jnp.float32)

    def late(step, side):
        chunk = order[step] * 2 + side

        def body(i, carry):
            at = pl.ds(pl.multiple_of(i * group * SUB, SUB), group * SUB)
            state = tuple(parts[chunk, c, at, :].reshape(group, SUB, LANE) for c in range(4))
            there = behind[step, window(side * share + i * group), :]
            put(chunk, i * group, plane_step(planes - 1, chunk * share + i * group, state, there))
            return carry

        lax.fori_loop(0, per_share, body, 0)

    in_front = core == 0
    pair_copies = []
    piece_copies = []
    ahead = 2
    for step in range(min(ahead, chips)):
        early(step)
    for step, q in enumerate(order):
        arrive(step)
        late(step, 1 - core)
        copy = remote(
            parts.at[q * 2 + (1 - core)], pair.at[step], pair_send_sem.at[step], pair_recv_sem.at[step], partner, tile
        )
        copy.start()
        pair_copies.append(copy)
        late(step, core)
        if step + ahead < chips:
            early(step + ahead)
        copy.wait_recv()
        chunk = q * 2 + core
        mine = [parts[chunk, c] for c in range(4)]
        theirs = [pair[step, c] for c in range(4)]
        near_through = jnp.where(in_front, mine[3], theirs[3])
        final = step == chips - 1
        target = pieces.at[chip] if final else send.at[step]
        for c in range(3):
            target[c] = jnp.where(in_front, mine[c], theirs[c]) + near_through * jnp.where(in_front, theirs[c], mine[c])
        target[3] = mine[3] * theirs[3]
        if not final:
            copy = remote(
                send.at[step], pieces.at[chip], piece_send_sem.at[step], piece_recv_sem.at[step],
                q * 2 + core, tile,
            )
            copy.start()
            piece_copies.append(copy)

    for copy in piece_copies:
        copy.wait_recv()
    colour = [pieces[0, c] for c in range(3)]
    through = pieces[0, 3]
    for k in range(1, chips):
        colour = [colour[c] + through * pieces[k, c] for c in range(3)]
        through = through * pieces[k, 3]
    image = (0.5 * (colour[0] + colour[1]), colour[2], 0.5 * (colour[0] - colour[1]), 1.0 - through)
    for c in range(4):
        result[:, c * SUB : (c + 1) * SUB, :] = image[c].reshape(share, SUB, LANE)
    for j in range(cols // LANE):
        out[:, :, j * LANE : (j + 1) * LANE] = result[:, pl.ds(j, 4, stride=SUB), :]

    for copy in pair_copies + piece_copies:
        copy.wait_send()
    for cond, copy in edges + sends:
        @pl.when(cond)
        def _(copy=copy):
            copy.wait_send()


def local(field):
    planes, rows, cols = field.shape
    depth_count = lax.axis_size("depth")
    chips = depth_count // 2
    share = rows // depth_count
    f32 = jnp.float32
    dims = (planes, rows, cols, depth_count, lax.axis_size("tile"))
    dma = pltpu.SemaphoreType.DMA
    image = pl.pallas_call(
        functools.partial(kernel, dims),
        out_shape=jax.ShapeDtypeStruct((share, 4, cols), f32),
        in_specs=[pl.BlockSpec(memory_space=pl.ANY)],
        out_specs=pl.BlockSpec(memory_space=pltpu.VMEM),
        scratch_shapes=[
            pltpu.VMEM((planes, rows, cols), f32),
            pltpu.VMEM((chips, (2 * share + 2) * SUB, LANE), f32),
            pltpu.VMEM((planes, (rows + 2) * SUB, LANE), f32),
            pltpu.VMEM((planes, SUB, LANE), f32),
            pltpu.VMEM((planes, SUB, LANE), f32),
            pltpu.VMEM((planes + 1, SUB, LANE), f32),
            pltpu.VMEM((planes + 1, SUB, LANE), f32),
            pltpu.VMEM((depth_count, 4, share * SUB, LANE), f32),
            pltpu.VMEM((chips, 4, share * SUB, LANE), f32),
            pltpu.VMEM((chips, 4, share * SUB, LANE), f32),
            pltpu.VMEM((chips, 4, share * SUB, LANE), f32),
            pltpu.VMEM((share, 4 * SUB, LANE), f32),
            dma((planes,)),
            dma((chips, 3)),
            dma((chips, 3)),
            dma((4,)),
            dma((4,)),
            dma((chips,)),
            dma((chips,)),
            dma((chips,)),
            dma((chips,)),
        ],
        compiler_params=pltpu.CompilerParams(collective_id=0, has_side_effects=True),
    )(field)
    return jnp.transpose(image, (1, 0, 2))


def solution(mesh):
    return jax.shard_map(
        local,
        mesh=mesh,
        in_specs=(P("depth", "tile", None),),
        out_specs=P(None, ("tile", "depth"), None),
        check_vma=False,
    )
```

```python
import functools
import math

import jax
import jax.numpy as jnp
from jax import lax
from jax.experimental import pallas as pl
from jax.experimental.pallas import tpu as pltpu
from jax.sharding import PartitionSpec as P

centres = (-1.2, 0.3, 1.5)
spreads = (0.25, 0.35, 0.3)
heights = (2.0, 1.0, 3.0)
floor_density = 0.05
light_cols = 0.48
light_rows = 0.6
light_depth = 0.64

LOG2E = math.log2(math.e)
SUB, LANE = 8, 128


def kernel(
    dims, field, out, raw, behind, grid, low_send, high_send, low, high,
    parts, pair, send, pieces, result,
    raw_sem, plane_send_sem, plane_recv_sem, edge_send_sem, edge_recv_sem, pair_send_sem, pair_recv_sem,
    piece_send_sem, piece_recv_sem,
):
    planes, rows, cols, depth_count, tile_count = dims
    chips = depth_count // 2
    share = rows // depth_count
    spacing = 3.0 / (planes * depth_count)
    group = max(g for g in range(1, 5) if share % g == 0)
    me = lax.axis_index("depth")
    tile = lax.axis_index("tile")
    chip = me // 2
    core = me % 2
    partner = chip * 2 + (1 - core)

    def remote(src, dst, send_sem, recv_sem, depth_to, tile_to):
        return pltpu.make_async_remote_copy(
            src_ref=src, dst_ref=dst, send_sem=send_sem, recv_sem=recv_sem,
            device_id=(depth_to, tile_to), device_id_type=pl.DeviceIdType.MESH,
        )

    loads = [pltpu.make_async_copy(field.at[p], raw.at[p], raw_sem.at[p]) for p in range(planes)]
    for load in loads:
        load.start()

    has_front = me > 0
    has_behind = me < depth_count - 1
    has_low = tile > 0
    has_high = tile < tile_count - 1
    near = [
        (has_front, me - 1, tile),
        (has_behind, me + 1, tile),
        (has_low, me, tile - 1),
        (has_high, me, tile + 1),
        (has_front & has_low, me - 1, tile - 1),
        (has_front & has_high, me - 1, tile + 1),
        (has_behind & has_low, me + 1, tile - 1),
        (has_behind & has_high, me + 1, tile + 1),
    ]
    barrier = pltpu.get_barrier_semaphore()
    for cond, d, t in near:
        @pl.when(cond)
        def _(d=d, t=t):
            pl.semaphore_signal(barrier, inc=1, device_id=(d, t), device_id_type=pl.DeviceIdType.MESH)
    pl.semaphore_signal(barrier, inc=1, device_id=(partner, tile), device_id_type=pl.DeviceIdType.MESH)
    for step in range(chips - 1):
        other = (chip + step + 1) % chips * 2 + core
        pl.semaphore_signal(barrier, inc=1, device_id=(other, tile), device_id_type=pl.DeviceIdType.MESH)
    def spread(source, p):
        for r in range(0, rows, SUB):
            for j in range(cols // LANE):
                grid[p, pl.ds((r + 1) * SUB + j, SUB, stride=SUB), :] = source[
                    r : r + SUB, j * LANE : (j + 1) * LANE
                ]

    first, last = pl.ds(SUB, SUB), pl.ds(rows * SUB, SUB)
    for p in range(planes):
        loads[p].wait()
        spread(raw.at[p], p)
        low_send[p] = grid[p, first, :]
        high_send[p] = grid[p, last, :]

    greeted = chips
    for cond, _, _ in near:
        greeted = greeted + cond.astype(jnp.int32)
    pl.semaphore_wait(barrier, greeted)

    block = 2 * share
    sends = []

    def plane_row(row, count):
        return grid.at[0, pl.ds(pl.multiple_of((row + 1) * SUB, SUB), count * SUB), :]

    strips = []
    for step in range(chips):
        q = ((me + depth_count - 1) // 2 + step + 1) % chips
        strip = []
        for k, (cond, row, count, place) in enumerate((
            (has_front, q * block, block, 1),
            (has_front & (q > 0), jnp.maximum(q * block - 1, 0), 1, 0),
            (has_front & (q < chips - 1), jnp.minimum((q + 1) * block, rows - 1), 1, block + 1),
        )):
            copy = remote(
                plane_row(row, count), behind.at[step, pl.ds(place * SUB, count * SUB), :],
                plane_send_sem.at[step, k], plane_recv_sem.at[step, k], me - 1, tile,
            )
            sends.append((cond, copy))
            strip.append(copy)
        strips.append(strip)
    own = pl.ds(0, planes)
    to_low = remote(low_send, high.at[own], edge_send_sem.at[0], edge_recv_sem.at[0], me, tile - 1)
    to_high = remote(high_send, low.at[own], edge_send_sem.at[1], edge_recv_sem.at[1], me, tile + 1)
    corner_low = remote(
        low_send.at[0], high.at[planes], edge_send_sem.at[2], edge_recv_sem.at[2], me - 1, tile - 1
    )
    corner_high = remote(
        high_send.at[0], low.at[planes], edge_send_sem.at[3], edge_recv_sem.at[3], me - 1, tile + 1
    )
    edges = [
        (has_low, to_low),
        (has_high, to_high),
        (has_front & has_low, corner_low),
        (has_front & has_high, corner_high),
    ]
    for cond, copy in edges + sends:
        @pl.when(cond)
        def _(copy=copy):
            copy.start()

    below, above = pl.ds(0, SUB), pl.ds((rows + 1) * SUB, SUB)
    blank = jnp.zeros((SUB, LANE), jnp.float32)

    def fill(cond, copy, where, halo, which):
        @pl.when(cond)
        def _():
            copy.wait_recv()
            for p in which:
                grid[p, where, :] = halo[p]

        @pl.when(jnp.logical_not(cond))
        def _():
            for p in which:
                grid[p, where, :] = blank

    lane = lax.broadcasted_iota(jnp.int32, (group, SUB, LANE), 2)
    sub = lax.broadcasted_iota(jnp.int32, (group, SUB, LANE), 1)
    left_edge = lane == 0
    right_edge = lane == LANE - 1
    left_end = left_edge & (sub == 0)
    right_end = right_edge & (sub == SUB - 1)
    scale = spacing * LOG2E

    def plane_step(p, row, state, there):
        red, blue, green, through = state
        at = pl.ds(pl.multiple_of(row * SUB, SUB), (group + 2) * SUB)
        here = grid[p, at, :].reshape(group + 2, SUB, LANE)
        there = there.reshape(group + 2, SUB, LANE)
        total = here + there
        twice = total[1:-1]
        d_depth = there[1:-1] - here[1:-1]
        d_rows = total[2:] - total[:-2]
        from_left = pltpu.roll(twice, 1, 2)
        from_left = jnp.where(left_edge, pltpu.roll(from_left, 1, 1), from_left)
        from_left = jnp.where(left_end, 0.0, from_left)
        from_right = pltpu.roll(twice, LANE - 1, 2)
        from_right = jnp.where(right_edge, pltpu.roll(from_right, SUB - 1, 1), from_right)
        from_right = jnp.where(right_end, 0.0, from_right)
        d_cols = from_right - from_left
        facing = (0.25 * light_cols) * d_cols + (0.25 * light_rows) * d_rows + light_depth * d_depth
        length = (d_cols * d_cols + d_rows * d_rows) * 0.0625 + (d_depth * d_depth + 1.0)
        shading = 0.3 + 0.7 * jnp.abs(facing) * lax.rsqrt(length)
        optics = scale * floor_density
        for centre, width, bump in zip(centres, spreads, heights):
            root = math.sqrt(LOG2E) / width
            scaled = (0.5 * root) * twice - root * centre
            optics = optics + jnp.exp2(math.log2(bump * scale) - scaled * scaled)
        after = through * jnp.exp2(-optics)
        lit = (through - after) * shading
        middle = jnp.exp2((twice * (-0.25 * LOG2E)) * twice)
        balance = jnp.tanh(0.5 * twice)
        return (red + lit, blue + lit * balance, green + lit * middle, after)

    width = share * SUB

    def put(chunk, offset, state):
        at = pl.ds(pl.multiple_of(offset * SUB, SUB), group * SUB)
        for c in range(4):
            parts[chunk, c, at, :] = state[c].reshape(group * SUB, LANE)

    zero = jnp.zeros((group, SUB, LANE), jnp.float32)
    per_share = share // group

    def window(row):
        return pl.ds(pl.multiple_of(row * SUB, SUB), (group + 2) * SUB)

    order = [(chip + step + 1) % chips for step in range(chips)]

    def early(i, carry):
        state = (zero, zero, zero, zero + 1.0)
        for p in range(planes - 1):
            state = plane_step(p, i * group, state, grid[p + 1, window(i * group), :])
        put(i // per_share, i % per_share * group, state)
        return carry

    def end(step, cond, have, copy, halo, place):
        at = pl.ds(place * SUB, SUB)

        @pl.when(cond & have)
        def _():
            copy.wait_recv()
            behind[step, at, :] = halo[planes]

        @pl.when(cond & jnp.logical_not(have))
        def _():
            behind[step, at, :] = blank

    def arrive(step):
        q = order[step]
        whole, lower, upper = strips[step]

        @pl.when(has_behind)
        def _():
            whole.wait_recv()

        @pl.when(has_behind & (q > 0))
        def _():
            lower.wait_recv()

        @pl.when(has_behind & (q < chips - 1))
        def _():
            upper.wait_recv()

        end(step, has_behind & (q == 0), has_low, corner_high, low, 0)
        end(step, has_behind & (q == chips - 1), has_high, corner_low, high, block + 1)

        @pl.when(jnp.logical_not(has_behind))
        def _():
            behind[step] = jnp.zeros(behind.shape[1:], jnp.float32)

    def late(step, side):
        chunk = order[step] * 2 + side

        def body(i, carry):
            at = pl.ds(pl.multiple_of(i * group * SUB, SUB), group * SUB)
            state = tuple(parts[chunk, c, at, :].reshape(group, SUB, LANE) for c in range(4))
            there = behind[step, window(side * share + i * group), :]
            put(chunk, i * group, plane_step(planes - 1, chunk * share + i * group, state, there))
            return carry

        lax.fori_loop(0, per_share, body, 0)

    groups = rows // group
    lax.fori_loop(1, groups - 1, early, 0)
    fill(has_high, to_low, above, high, range(planes))
    fill(has_low, to_high, below, low, range(planes))
    lax.fori_loop(0, 2, lambda i, carry: early(i * (groups - 1), carry), 0)

    in_front = core == 0
    pair_copies = []
    piece_copies = []

    def combine(step):
        q = order[step]
        pair_copies[step].wait_recv()
        chunk = q * 2 + core
        mine = [parts[chunk, c] for c in range(4)]
        theirs = [pair[step, c] for c in range(4)]
        near_through = jnp.where(in_front, mine[3], theirs[3])
        final = step == chips - 1
        target = pieces.at[chip] if final else send.at[step]
        for c in range(3):
            target[c] = jnp.where(in_front, mine[c], theirs[c]) + near_through * jnp.where(in_front, theirs[c], mine[c])
        target[3] = mine[3] * theirs[3]
        if not final:
            copy = remote(
                send.at[step], pieces.at[chip], piece_send_sem.at[step], piece_recv_sem.at[step],
                q * 2 + core, tile,
            )
            copy.start()
            piece_copies.append(copy)

    for step, q in enumerate(order):
        arrive(step)
        late(step, 1 - core)
        copy = remote(
            parts.at[q * 2 + (1 - core)], pair.at[step], pair_send_sem.at[step], pair_recv_sem.at[step], partner, tile
        )
        copy.start()
        pair_copies.append(copy)
        late(step, core)
        if step > 0:
            combine(step - 1)
    combine(chips - 1)

    for copy in piece_copies:
        copy.wait_recv()
    colour = [pieces[0, c] for c in range(3)]
    through = pieces[0, 3]
    for k in range(1, chips):
        colour = [colour[c] + through * pieces[k, c] for c in range(3)]
        through = through * pieces[k, 3]
    image = (0.5 * (colour[0] + colour[1]), colour[2], 0.5 * (colour[0] - colour[1]), through)
    for c in range(4):
        result[:, c * SUB : (c + 1) * SUB, :] = image[c].reshape(share, SUB, LANE)
    for j in range(cols // LANE):
        out[:, :, j * LANE : (j + 1) * LANE] = result[:, pl.ds(j, 4, stride=SUB), :]

    for copy in pair_copies + piece_copies:
        copy.wait_send()
    for cond, copy in edges + sends:
        @pl.when(cond)
        def _(copy=copy):
            copy.wait_send()


def local(field):
    planes, rows, cols = field.shape
    depth_count = lax.axis_size("depth")
    chips = depth_count // 2
    share = rows // depth_count
    f32 = jnp.float32
    dims = (planes, rows, cols, depth_count, lax.axis_size("tile"))
    dma = pltpu.SemaphoreType.DMA
    image = pl.pallas_call(
        functools.partial(kernel, dims),
        out_shape=jax.ShapeDtypeStruct((share, 4, cols), f32),
        in_specs=[pl.BlockSpec(memory_space=pl.ANY)],
        out_specs=pl.BlockSpec(memory_space=pltpu.VMEM),
        scratch_shapes=[
            pltpu.VMEM((planes, rows, cols), f32),
            pltpu.VMEM((chips, (2 * share + 2) * SUB, LANE), f32),
            pltpu.VMEM((planes, (rows + 2) * SUB, LANE), f32),
            pltpu.VMEM((planes, SUB, LANE), f32),
            pltpu.VMEM((planes, SUB, LANE), f32),
            pltpu.VMEM((planes + 1, SUB, LANE), f32),
            pltpu.VMEM((planes + 1, SUB, LANE), f32),
            pltpu.VMEM((depth_count, 4, share * SUB, LANE), f32),
            pltpu.VMEM((chips, 4, share * SUB, LANE), f32),
            pltpu.VMEM((chips, 4, share * SUB, LANE), f32),
            pltpu.VMEM((chips, 4, share * SUB, LANE), f32),
            pltpu.VMEM((share, 4 * SUB, LANE), f32),
            dma((planes,)),
            dma((chips, 3)),
            dma((chips, 3)),
            dma((4,)),
            dma((4,)),
            dma((chips,)),
            dma((chips,)),
            dma((chips,)),
            dma((chips,)),
        ],
        compiler_params=pltpu.CompilerParams(collective_id=0, has_side_effects=True),
    )(field)
    image = jnp.transpose(image, (1, 0, 2))
    channel = lax.broadcasted_iota(jnp.int32, image.shape, 0)
    return jnp.where(channel == 3, 1.0 - image, image)


def solution(mesh):
    return jax.shard_map(
        local,
        mesh=mesh,
        in_specs=(P("depth", "tile", None),),
        out_specs=P(None, ("tile", "depth"), None),
        check_vma=False,
    )
```

```python
import functools
import math

import jax
import jax.numpy as jnp
from jax import lax
from jax.experimental import pallas as pl
from jax.experimental.pallas import tpu as pltpu
from jax.sharding import PartitionSpec as P

centres = (-1.2, 0.3, 1.5)
spreads = (0.25, 0.35, 0.3)
heights = (2.0, 1.0, 3.0)
floor_density = 0.05
light_cols = 0.48
light_rows = 0.6
light_depth = 0.64

LOG2E = math.log2(math.e)
SUB, LANE = 8, 128


def kernel(
    dims, field, out, raw, behind, grid, low_send, high_send, low, high,
    parts, pair, send, pieces, result,
    raw_sem, plane_send_sem, plane_recv_sem, edge_send_sem, edge_recv_sem, pair_send_sem, pair_recv_sem,
    piece_send_sem, piece_recv_sem,
):
    planes, rows, cols, depth_count, tile_count = dims
    chips = depth_count // 2
    share = rows // depth_count
    spacing = 3.0 / (planes * depth_count)
    group = max(g for g in range(1, 5) if share % g == 0)
    me = lax.axis_index("depth")
    tile = lax.axis_index("tile")
    chip = me // 2
    core = me % 2
    partner = chip * 2 + (1 - core)

    def remote(src, dst, send_sem, recv_sem, depth_to, tile_to):
        return pltpu.make_async_remote_copy(
            src_ref=src, dst_ref=dst, send_sem=send_sem, recv_sem=recv_sem,
            device_id=(depth_to, tile_to), device_id_type=pl.DeviceIdType.MESH,
        )

    loads = [pltpu.make_async_copy(field.at[p], raw.at[p], raw_sem.at[p]) for p in range(planes)]
    for load in loads:
        load.start()

    has_front = me > 0
    has_behind = me < depth_count - 1
    has_low = tile > 0
    has_high = tile < tile_count - 1
    near = [
        (has_front, me - 1, tile),
        (has_behind, me + 1, tile),
        (has_low, me, tile - 1),
        (has_high, me, tile + 1),
        (has_front & has_low, me - 1, tile - 1),
        (has_front & has_high, me - 1, tile + 1),
        (has_behind & has_low, me + 1, tile - 1),
        (has_behind & has_high, me + 1, tile + 1),
    ]
    barrier = pltpu.get_barrier_semaphore()
    for cond, d, t in near:
        @pl.when(cond)
        def _(d=d, t=t):
            pl.semaphore_signal(barrier, inc=1, device_id=(d, t), device_id_type=pl.DeviceIdType.MESH)
    pl.semaphore_signal(barrier, inc=1, device_id=(partner, tile), device_id_type=pl.DeviceIdType.MESH)
    for step in range(chips - 1):
        other = (chip + step + 1) % chips * 2 + core
        pl.semaphore_signal(barrier, inc=1, device_id=(other, tile), device_id_type=pl.DeviceIdType.MESH)
    def spread(source, p):
        for r in range(0, rows, SUB):
            for j in range(cols // LANE):
                grid[p, pl.ds((r + 1) * SUB + j, SUB, stride=SUB), :] = source[
                    r : r + SUB, j * LANE : (j + 1) * LANE
                ]

    first, last = pl.ds(SUB, SUB), pl.ds(rows * SUB, SUB)
    for p in range(planes):
        loads[p].wait()
        spread(raw.at[p], p)
        low_send[p] = grid[p, first, :]
        high_send[p] = grid[p, last, :]

    greeted = chips
    for cond, _, _ in near:
        greeted = greeted + cond.astype(jnp.int32)
    pl.semaphore_wait(barrier, greeted)

    block = 2 * share
    sends = []

    def plane_row(row, count):
        return grid.at[0, pl.ds(pl.multiple_of((row + 1) * SUB, SUB), count * SUB), :]

    strips = []
    for step in range(chips):
        q = ((me + depth_count - 1) // 2 + step + 1) % chips
        strip = []
        for k, (cond, row, count, place) in enumerate((
            (has_front, q * block, block, 1),
            (has_front & (q > 0), jnp.maximum(q * block - 1, 0), 1, 0),
            (has_front & (q < chips - 1), jnp.minimum((q + 1) * block, rows - 1), 1, block + 1),
        )):
            copy = remote(
                plane_row(row, count), behind.at[step, pl.ds(place * SUB, count * SUB), :],
                plane_send_sem.at[step, k], plane_recv_sem.at[step, k], me - 1, tile,
            )
            sends.append((cond, copy))
            strip.append(copy)
        strips.append(strip)
    own = pl.ds(0, planes)
    to_low = remote(low_send, high.at[own], edge_send_sem.at[0], edge_recv_sem.at[0], me, tile - 1)
    to_high = remote(high_send, low.at[own], edge_send_sem.at[1], edge_recv_sem.at[1], me, tile + 1)
    corner_low = remote(
        low_send.at[0], high.at[planes], edge_send_sem.at[2], edge_recv_sem.at[2], me - 1, tile - 1
    )
    corner_high = remote(
        high_send.at[0], low.at[planes], edge_send_sem.at[3], edge_recv_sem.at[3], me - 1, tile + 1
    )
    edges = [
        (has_low, to_low),
        (has_high, to_high),
        (has_front & has_low, corner_low),
        (has_front & has_high, corner_high),
    ]
    for cond, copy in edges + sends:
        @pl.when(cond)
        def _(copy=copy):
            copy.start()

    below, above = pl.ds(0, SUB), pl.ds((rows + 1) * SUB, SUB)
    blank = jnp.zeros((SUB, LANE), jnp.float32)

    def fill(cond, copy, where, halo, which):
        @pl.when(cond)
        def _():
            copy.wait_recv()
            for p in which:
                grid[p, where, :] = halo[p]

        @pl.when(jnp.logical_not(cond))
        def _():
            for p in which:
                grid[p, where, :] = blank

    lane = lax.broadcasted_iota(jnp.int32, (group, SUB, LANE), 2)
    sub = lax.broadcasted_iota(jnp.int32, (group, SUB, LANE), 1)
    left_edge = lane == 0
    right_edge = lane == LANE - 1
    left_end = left_edge & (sub == 0)
    right_end = right_edge & (sub == SUB - 1)
    scale = spacing * LOG2E

    def plane_step(p, row, state, there):
        red, blue, green, through = state
        at = pl.ds(pl.multiple_of(row * SUB, SUB), (group + 2) * SUB)
        here = grid[p, at, :].reshape(group + 2, SUB, LANE)
        there = there.reshape(group + 2, SUB, LANE)
        total = here + there
        twice = total[1:-1]
        d_depth = there[1:-1] - here[1:-1]
        d_rows = total[2:] - total[:-2]
        from_left = pltpu.roll(twice, 1, 2)
        from_left = jnp.where(left_edge, pltpu.roll(from_left, 1, 1), from_left)
        from_left = jnp.where(left_end, 0.0, from_left)
        from_right = pltpu.roll(twice, LANE - 1, 2)
        from_right = jnp.where(right_edge, pltpu.roll(from_right, SUB - 1, 1), from_right)
        from_right = jnp.where(right_end, 0.0, from_right)
        d_cols = from_right - from_left
        facing = (0.25 * light_cols) * d_cols + (0.25 * light_rows) * d_rows + light_depth * d_depth
        length = (d_cols * d_cols + d_rows * d_rows) * 0.0625 + (d_depth * d_depth + 1.0)
        shading = 0.3 + 0.7 * jnp.abs(facing) * lax.rsqrt(length)
        optics = scale * floor_density
        for centre, width, bump in zip(centres, spreads, heights):
            root = math.sqrt(LOG2E) / width
            scaled = (0.5 * root) * twice - root * centre
            optics = optics + jnp.exp2(math.log2(bump * scale) - scaled * scaled)
        after = through * jnp.exp2(-optics)
        lit = (through - after) * shading
        middle = jnp.exp2((twice * (-0.25 * LOG2E)) * twice)
        balance = jnp.tanh(0.5 * twice)
        return (red + lit, blue + lit * balance, green + lit * middle, after)

    width = share * SUB

    def put(chunk, offset, state):
        at = pl.ds(pl.multiple_of(offset * SUB, SUB), group * SUB)
        for c in range(4):
            parts[chunk, c, at, :] = state[c].reshape(group * SUB, LANE)

    zero = jnp.zeros((group, SUB, LANE), jnp.float32)
    per_share = share // group

    def window(row):
        return pl.ds(pl.multiple_of(row * SUB, SUB), (group + 2) * SUB)

    order = [(chip + step + 1) % chips for step in range(chips)]

    def early(i, carry):
        state = (zero, zero, zero, zero + 1.0)
        for p in range(planes - 1):
            state = plane_step(p, i * group, state, grid[p + 1, window(i * group), :])
        put(i // per_share, i % per_share * group, state)
        return carry

    def end(step, cond, have, copy, halo, place):
        at = pl.ds(place * SUB, SUB)

        @pl.when(cond & have)
        def _():
            copy.wait_recv()
            behind[step, at, :] = halo[planes]

        @pl.when(cond & jnp.logical_not(have))
        def _():
            behind[step, at, :] = blank

    def arrive(step):
        q = order[step]
        whole, lower, upper = strips[step]

        @pl.when(has_behind)
        def _():
            whole.wait_recv()

        @pl.when(has_behind & (q > 0))
        def _():
            lower.wait_recv()

        @pl.when(has_behind & (q < chips - 1))
        def _():
            upper.wait_recv()

        end(step, has_behind & (q == 0), has_low, corner_high, low, 0)
        end(step, has_behind & (q == chips - 1), has_high, corner_low, high, block + 1)

        @pl.when(jnp.logical_not(has_behind))
        def _():
            behind[step] = jnp.zeros(behind.shape[1:], jnp.float32)

    def late(step, side):
        chunk = order[step] * 2 + side

        def body(i, carry):
            at = pl.ds(pl.multiple_of(i * group * SUB, SUB), group * SUB)
            state = tuple(parts[chunk, c, at, :].reshape(group, SUB, LANE) for c in range(4))
            there = behind[step, window(side * share + i * group), :]
            put(chunk, i * group, plane_step(planes - 1, chunk * share + i * group, state, there))
            return carry

        lax.fori_loop(0, per_share, body, 0)

    groups = rows // group
    lax.fori_loop(1, groups - 1, early, 0)
    fill(has_high, to_low, above, high, range(planes))
    fill(has_low, to_high, below, low, range(planes))
    lax.fori_loop(0, 2, lambda i, carry: early(i * (groups - 1), carry), 0)

    in_front = core == 0
    pair_copies = []
    piece_copies = []

    def combine(step):
        q = order[step]
        pair_copies[step].wait_recv()
        chunk = q * 2 + core
        mine = [parts[chunk, c] for c in range(4)]
        theirs = [pair[step, c] for c in range(4)]
        near_through = jnp.where(in_front, mine[3], theirs[3])
        final = step == chips - 1
        target = pieces.at[chip] if final else send.at[step]
        for c in range(3):
            target[c] = jnp.where(in_front, mine[c], theirs[c]) + near_through * jnp.where(in_front, theirs[c], mine[c])
        target[3] = mine[3] * theirs[3]
        if not final:
            copy = remote(
                send.at[step], pieces.at[chip], piece_send_sem.at[step], piece_recv_sem.at[step],
                q * 2 + core, tile,
            )
            copy.start()
            piece_copies.append(copy)

    for step, q in enumerate(order):
        arrive(step)
        late(step, 1 - core)
        copy = remote(
            parts.at[q * 2 + (1 - core)], pair.at[step], pair_send_sem.at[step], pair_recv_sem.at[step], partner, tile
        )
        copy.start()
        pair_copies.append(copy)
        late(step, core)
        if step > 0:
            combine(step - 1)
    combine(chips - 1)

    for copy in piece_copies:
        copy.wait_recv()
    colour = [pieces[0, c] for c in range(3)]
    through = pieces[0, 3]
    for k in range(1, chips):
        colour = [colour[c] + through * pieces[k, c] for c in range(3)]
        through = through * pieces[k, 3]
    image = (0.5 * (colour[0] + colour[1]), colour[2], 0.5 * (colour[0] - colour[1]), through)
    for c in range(4):
        result[:, c * SUB : (c + 1) * SUB, :] = image[c].reshape(share, SUB, LANE)
    for j in range(cols // LANE):
        out[:, :, j * LANE : (j + 1) * LANE] = result[:, pl.ds(j, 4, stride=SUB), :]

    for copy in pair_copies + piece_copies:
        copy.wait_send()
    for cond, copy in edges + sends:
        @pl.when(cond)
        def _(copy=copy):
            copy.wait_send()


def local(field):
    planes, rows, cols = field.shape
    depth_count = lax.axis_size("depth")
    chips = depth_count // 2
    share = rows // depth_count
    f32 = jnp.float32
    dims = (planes, rows, cols, depth_count, lax.axis_size("tile"))
    dma = pltpu.SemaphoreType.DMA
    image = pl.pallas_call(
        functools.partial(kernel, dims),
        out_shape=jax.ShapeDtypeStruct((share, 4, cols), f32),
        in_specs=[pl.BlockSpec(memory_space=pltpu.HBM)],
        out_specs=pl.BlockSpec(memory_space=pltpu.VMEM),
        scratch_shapes=[
            pltpu.VMEM((planes, rows, cols), f32),
            pltpu.VMEM((chips, (2 * share + 2) * SUB, LANE), f32),
            pltpu.VMEM((planes, (rows + 2) * SUB, LANE), f32),
            pltpu.VMEM((planes, SUB, LANE), f32),
            pltpu.VMEM((planes, SUB, LANE), f32),
            pltpu.VMEM((planes + 1, SUB, LANE), f32),
            pltpu.VMEM((planes + 1, SUB, LANE), f32),
            pltpu.VMEM((depth_count, 4, share * SUB, LANE), f32),
            pltpu.VMEM((chips, 4, share * SUB, LANE), f32),
            pltpu.VMEM((chips, 4, share * SUB, LANE), f32),
            pltpu.VMEM((chips, 4, share * SUB, LANE), f32),
            pltpu.VMEM((share, 4 * SUB, LANE), f32),
            dma((planes,)),
            dma((chips, 3)),
            dma((chips, 3)),
            dma((4,)),
            dma((4,)),
            dma((chips,)),
            dma((chips,)),
            dma((chips,)),
            dma((chips,)),
        ],
        compiler_params=pltpu.CompilerParams(
            collective_id=0, has_side_effects=True, vmem_limit_bytes=55_000_000
        ),
    )(field)
    image = jnp.transpose(image, (1, 0, 2))
    channel = lax.broadcasted_iota(jnp.int32, image.shape, 0)
    return jnp.where(channel == 3, 1.0 - image, image)


def solution(mesh):
    return jax.shard_map(
        local,
        mesh=mesh,
        in_specs=(P("depth", "tile", None),),
        out_specs=P(None, ("tile", "depth"), None),
        check_vma=False,
    )
```

```python
import functools
import math

import jax
import jax.numpy as jnp
from jax import lax
from jax.experimental import pallas as pl
from jax.experimental.pallas import tpu as pltpu
from jax.sharding import PartitionSpec as P

centres = (-1.2, 0.3, 1.5)
spreads = (0.25, 0.35, 0.3)
heights = (2.0, 1.0, 3.0)
floor_density = 0.05
light_cols = 0.48
light_rows = 0.6
light_depth = 0.64

LOG2E = math.log2(math.e)
SUB, LANE = 8, 128


def kernel(
    dims, field, out, raw, behind, grid, low_send, high_send, low, high,
    parts, pair, send, pieces, result,
    raw_sem, plane_send_sem, plane_recv_sem, edge_send_sem, edge_recv_sem, pair_send_sem, pair_recv_sem,
    piece_send_sem, piece_recv_sem,
):
    planes, rows, cols, depth_count, tile_count = dims
    chips = depth_count // 2
    share = rows // depth_count
    spacing = 3.0 / (planes * depth_count)
    group = max(g for g in range(1, 5) if share % g == 0)
    me = lax.axis_index("depth")
    tile = lax.axis_index("tile")
    chip = me // 2
    core = me % 2
    partner = chip * 2 + (1 - core)

    def remote(src, dst, send_sem, recv_sem, depth_to, tile_to):
        return pltpu.make_async_remote_copy(
            src_ref=src, dst_ref=dst, send_sem=send_sem, recv_sem=recv_sem,
            device_id=(depth_to, tile_to), device_id_type=pl.DeviceIdType.MESH,
        )

    loads = [pltpu.make_async_copy(field.at[p], raw.at[p], raw_sem.at[p]) for p in range(planes)]
    for load in loads:
        load.start()

    has_front = me > 0
    has_behind = me < depth_count - 1
    has_low = tile > 0
    has_high = tile < tile_count - 1
    near = [
        (has_front, me - 1, tile),
        (has_behind, me + 1, tile),
        (has_low, me, tile - 1),
        (has_high, me, tile + 1),
        (has_front & has_low, me - 1, tile - 1),
        (has_front & has_high, me - 1, tile + 1),
        (has_behind & has_low, me + 1, tile - 1),
        (has_behind & has_high, me + 1, tile + 1),
    ]
    barrier = pltpu.get_barrier_semaphore()
    for cond, d, t in near:
        @pl.when(cond)
        def _(d=d, t=t):
            pl.semaphore_signal(barrier, inc=1, device_id=(d, t), device_id_type=pl.DeviceIdType.MESH)
    pl.semaphore_signal(barrier, inc=1, device_id=(partner, tile), device_id_type=pl.DeviceIdType.MESH)
    for step in range(chips - 1):
        other = (chip + step + 1) % chips * 2 + core
        pl.semaphore_signal(barrier, inc=1, device_id=(other, tile), device_id_type=pl.DeviceIdType.MESH)
    def spread(source, p):
        for r in range(0, rows, SUB):
            for j in range(cols // LANE):
                grid[p, pl.ds((r + 1) * SUB + j, SUB, stride=SUB), :] = source[
                    r : r + SUB, j * LANE : (j + 1) * LANE
                ]

    first, last = pl.ds(SUB, SUB), pl.ds(rows * SUB, SUB)
    for p in range(planes):
        loads[p].wait()
        spread(raw.at[p], p)
        low_send[p] = grid[p, first, :]
        high_send[p] = grid[p, last, :]

    greeted = chips
    for cond, _, _ in near:
        greeted = greeted + cond.astype(jnp.int32)
    pl.semaphore_wait(barrier, greeted)

    block = 2 * share
    sends = []

    def plane_row(row, count):
        return grid.at[0, pl.ds(pl.multiple_of((row + 1) * SUB, SUB), count * SUB), :]

    def turn(at, step):
        return (at + (2 * (at % 2) - 1) * (step + 1) + chips) % chips

    strips = []
    for step in range(chips):
        q = turn((me + depth_count - 1) // 2 % chips, step)
        strip = []
        for k, (cond, row, count, place) in enumerate((
            (has_front, q * block, block, 1),
            (has_front & (q > 0), jnp.maximum(q * block - 1, 0), 1, 0),
            (has_front & (q < chips - 1), jnp.minimum((q + 1) * block, rows - 1), 1, block + 1),
        )):
            copy = remote(
                plane_row(row, count), behind.at[step, pl.ds(place * SUB, count * SUB), :],
                plane_send_sem.at[step, k], plane_recv_sem.at[step, k], me - 1, tile,
            )
            sends.append((cond, copy))
            strip.append(copy)
        strips.append(strip)
    own = pl.ds(0, planes)
    to_low = remote(low_send, high.at[own], edge_send_sem.at[0], edge_recv_sem.at[0], me, tile - 1)
    to_high = remote(high_send, low.at[own], edge_send_sem.at[1], edge_recv_sem.at[1], me, tile + 1)
    corner_low = remote(
        low_send.at[0], high.at[planes], edge_send_sem.at[2], edge_recv_sem.at[2], me - 1, tile - 1
    )
    corner_high = remote(
        high_send.at[0], low.at[planes], edge_send_sem.at[3], edge_recv_sem.at[3], me - 1, tile + 1
    )
    edges = [
        (has_low, to_low),
        (has_high, to_high),
        (has_front & has_low, corner_low),
        (has_front & has_high, corner_high),
    ]
    for cond, copy in edges + sends:
        @pl.when(cond)
        def _(copy=copy):
            copy.start()

    below, above = pl.ds(0, SUB), pl.ds((rows + 1) * SUB, SUB)
    blank = jnp.zeros((SUB, LANE), jnp.float32)

    def fill(cond, copy, where, halo, which):
        @pl.when(cond)
        def _():
            copy.wait_recv()
            for p in which:
                grid[p, where, :] = halo[p]

        @pl.when(jnp.logical_not(cond))
        def _():
            for p in which:
                grid[p, where, :] = blank

    lane = lax.broadcasted_iota(jnp.int32, (group, SUB, LANE), 2)
    sub = lax.broadcasted_iota(jnp.int32, (group, SUB, LANE), 1)
    left_edge = lane == 0
    right_edge = lane == LANE - 1
    left_end = left_edge & (sub == 0)
    right_end = right_edge & (sub == SUB - 1)
    scale = spacing * LOG2E

    def plane_step(p, row, state, there):
        red, blue, green, through = state
        at = pl.ds(pl.multiple_of(row * SUB, SUB), (group + 2) * SUB)
        here = grid[p, at, :].reshape(group + 2, SUB, LANE)
        there = there.reshape(group + 2, SUB, LANE)
        total = here + there
        twice = total[1:-1]
        d_depth = there[1:-1] - here[1:-1]
        d_rows = total[2:] - total[:-2]
        from_left = pltpu.roll(twice, 1, 2)
        from_left = jnp.where(left_edge, pltpu.roll(from_left, 1, 1), from_left)
        from_left = jnp.where(left_end, 0.0, from_left)
        from_right = pltpu.roll(twice, LANE - 1, 2)
        from_right = jnp.where(right_edge, pltpu.roll(from_right, SUB - 1, 1), from_right)
        from_right = jnp.where(right_end, 0.0, from_right)
        d_cols = from_right - from_left
        facing = (0.25 * light_cols) * d_cols + (0.25 * light_rows) * d_rows + light_depth * d_depth
        length = (d_cols * d_cols + d_rows * d_rows) * 0.0625 + (d_depth * d_depth + 1.0)
        shading = 0.3 + 0.7 * jnp.abs(facing) * lax.rsqrt(length)
        optics = scale * floor_density
        for centre, width, bump in zip(centres, spreads, heights):
            root = math.sqrt(LOG2E) / width
            scaled = (0.5 * root) * twice - root * centre
            optics = optics + jnp.exp2(math.log2(bump * scale) - scaled * scaled)
        after = through * jnp.exp2(-optics)
        lit = (through - after) * shading
        middle = jnp.exp2((twice * (-0.25 * LOG2E)) * twice)
        balance = jnp.tanh(0.5 * twice)
        return (red + lit, blue + lit * balance, green + lit * middle, after)

    width = share * SUB

    def put(chunk, offset, state):
        at = pl.ds(pl.multiple_of(offset * SUB, SUB), group * SUB)
        for c in range(4):
            parts[chunk, c, at, :] = state[c].reshape(group * SUB, LANE)

    zero = jnp.zeros((group, SUB, LANE), jnp.float32)
    per_share = share // group

    def window(row):
        return pl.ds(pl.multiple_of(row * SUB, SUB), (group + 2) * SUB)

    order = [turn(chip, step) for step in range(chips)]

    def early(i, carry):
        state = (zero, zero, zero, zero + 1.0)
        for p in range(planes - 1):
            state = plane_step(p, i * group, state, grid[p + 1, window(i * group), :])
        put(i // per_share, i % per_share * group, state)
        return carry

    def end(step, cond, have, copy, halo, place):
        at = pl.ds(place * SUB, SUB)

        @pl.when(cond & have)
        def _():
            copy.wait_recv()
            behind[step, at, :] = halo[planes]

        @pl.when(cond & jnp.logical_not(have))
        def _():
            behind[step, at, :] = blank

    def arrive(step):
        q = order[step]
        whole, lower, upper = strips[step]

        @pl.when(has_behind)
        def _():
            whole.wait_recv()

        @pl.when(has_behind & (q > 0))
        def _():
            lower.wait_recv()

        @pl.when(has_behind & (q < chips - 1))
        def _():
            upper.wait_recv()

        end(step, has_behind & (q == 0), has_low, corner_high, low, 0)
        end(step, has_behind & (q == chips - 1), has_high, corner_low, high, block + 1)

        @pl.when(jnp.logical_not(has_behind))
        def _():
            behind[step] = jnp.zeros(behind.shape[1:], jnp.float32)

    def late(step, side):
        chunk = order[step] * 2 + side

        def body(i, carry):
            at = pl.ds(pl.multiple_of(i * group * SUB, SUB), group * SUB)
            state = tuple(parts[chunk, c, at, :].reshape(group, SUB, LANE) for c in range(4))
            there = behind[step, window(side * share + i * group), :]
            put(chunk, i * group, plane_step(planes - 1, chunk * share + i * group, state, there))
            return carry

        lax.fori_loop(0, per_share, body, 0)

    groups = rows // group
    lax.fori_loop(1, groups - 1, early, 0)
    fill(has_high, to_low, above, high, range(planes))
    fill(has_low, to_high, below, low, range(planes))
    lax.fori_loop(0, 2, lambda i, carry: early(i * (groups - 1), carry), 0)

    in_front = core == 0
    pair_copies = []
    piece_copies = []

    def combine(step):
        q = order[step]
        pair_copies[step].wait_recv()
        chunk = q * 2 + core
        mine = [parts[chunk, c] for c in range(4)]
        theirs = [pair[step, c] for c in range(4)]
        near_through = jnp.where(in_front, mine[3], theirs[3])
        final = step == chips - 1
        target = pieces.at[chip] if final else send.at[step]
        for c in range(3):
            target[c] = jnp.where(in_front, mine[c], theirs[c]) + near_through * jnp.where(in_front, theirs[c], mine[c])
        target[3] = mine[3] * theirs[3]
        if not final:
            copy = remote(
                send.at[step], pieces.at[chip], piece_send_sem.at[step], piece_recv_sem.at[step],
                q * 2 + core, tile,
            )
            copy.start()
            piece_copies.append(copy)

    for step, q in enumerate(order):
        arrive(step)
        late(step, 1 - core)
        copy = remote(
            parts.at[q * 2 + (1 - core)], pair.at[step], pair_send_sem.at[step], pair_recv_sem.at[step], partner, tile
        )
        copy.start()
        pair_copies.append(copy)
        late(step, core)
        if step > 0:
            combine(step - 1)
    combine(chips - 1)

    for copy in piece_copies:
        copy.wait_recv()
    colour = [pieces[0, c] for c in range(3)]
    through = pieces[0, 3]
    for k in range(1, chips):
        colour = [colour[c] + through * pieces[k, c] for c in range(3)]
        through = through * pieces[k, 3]
    image = (0.5 * (colour[0] + colour[1]), colour[2], 0.5 * (colour[0] - colour[1]), through)
    for c in range(4):
        result[:, c * SUB : (c + 1) * SUB, :] = image[c].reshape(share, SUB, LANE)
    for j in range(cols // LANE):
        out[:, :, j * LANE : (j + 1) * LANE] = result[:, pl.ds(j, 4, stride=SUB), :]

    for copy in pair_copies + piece_copies:
        copy.wait_send()
    for cond, copy in edges + sends:
        @pl.when(cond)
        def _(copy=copy):
            copy.wait_send()


def local(field):
    planes, rows, cols = field.shape
    depth_count = lax.axis_size("depth")
    chips = depth_count // 2
    share = rows // depth_count
    f32 = jnp.float32
    dims = (planes, rows, cols, depth_count, lax.axis_size("tile"))
    dma = pltpu.SemaphoreType.DMA
    image = pl.pallas_call(
        functools.partial(kernel, dims),
        out_shape=jax.ShapeDtypeStruct((share, 4, cols), f32),
        in_specs=[pl.BlockSpec(memory_space=pltpu.HBM)],
        out_specs=pl.BlockSpec(memory_space=pltpu.VMEM),
        scratch_shapes=[
            pltpu.VMEM((planes, rows, cols), f32),
            pltpu.VMEM((chips, (2 * share + 2) * SUB, LANE), f32),
            pltpu.VMEM((planes, (rows + 2) * SUB, LANE), f32),
            pltpu.VMEM((planes, SUB, LANE), f32),
            pltpu.VMEM((planes, SUB, LANE), f32),
            pltpu.VMEM((planes + 1, SUB, LANE), f32),
            pltpu.VMEM((planes + 1, SUB, LANE), f32),
            pltpu.VMEM((depth_count, 4, share * SUB, LANE), f32),
            pltpu.VMEM((chips, 4, share * SUB, LANE), f32),
            pltpu.VMEM((chips, 4, share * SUB, LANE), f32),
            pltpu.VMEM((chips, 4, share * SUB, LANE), f32),
            pltpu.VMEM((share, 4 * SUB, LANE), f32),
            dma((planes,)),
            dma((chips, 3)),
            dma((chips, 3)),
            dma((4,)),
            dma((4,)),
            dma((chips,)),
            dma((chips,)),
            dma((chips,)),
            dma((chips,)),
        ],
        compiler_params=pltpu.CompilerParams(
            collective_id=0, has_side_effects=True, vmem_limit_bytes=55_000_000
        ),
    )(field)
    image = jnp.transpose(image, (1, 0, 2))
    channel = lax.broadcasted_iota(jnp.int32, image.shape, 0)
    return jnp.where(channel == 3, 1.0 - image, image)


def solution(mesh):
    return jax.shard_map(
        local,
        mesh=mesh,
        in_specs=(P("depth", "tile", None),),
        out_specs=P(None, ("tile", "depth"), None),
        check_vma=False,
    )
```

```python
import functools
import math

import jax
import jax.numpy as jnp
from jax import lax
from jax.experimental import pallas as pl
from jax.experimental.pallas import tpu as pltpu
from jax.sharding import PartitionSpec as P

centres = (-1.2, 0.3, 1.5)
spreads = (0.25, 0.35, 0.3)
heights = (2.0, 1.0, 3.0)
floor_density = 0.05
light_cols = 0.48
light_rows = 0.6
light_depth = 0.64

LOG2E = math.log2(math.e)
SUB, LANE = 8, 128


def kernel(
    dims, field, out, raw, behind, grid, low_send, high_send, low, high,
    parts, pair, send, pieces, result,
    raw_sem, plane_send_sem, plane_recv_sem, edge_send_sem, edge_recv_sem, pair_send_sem, pair_recv_sem,
    piece_send_sem, piece_recv_sem,
):
    planes, rows, cols, depth_count, tile_count = dims
    chips = depth_count // 2
    share = rows // depth_count
    spacing = 3.0 / (planes * depth_count)
    group = max(g for g in range(1, 5) if share % g == 0)
    me = lax.axis_index("depth")
    tile = lax.axis_index("tile")
    chip = me // 2
    core = me % 2
    partner = chip * 2 + (1 - core)

    def remote(src, dst, send_sem, recv_sem, depth_to, tile_to):
        return pltpu.make_async_remote_copy(
            src_ref=src, dst_ref=dst, send_sem=send_sem, recv_sem=recv_sem,
            device_id=(depth_to, tile_to), device_id_type=pl.DeviceIdType.MESH,
        )

    loads = [pltpu.make_async_copy(field.at[p], raw.at[p], raw_sem.at[p]) for p in range(planes)]
    for load in loads:
        load.start()

    has_front = me > 0
    has_behind = me < depth_count - 1
    has_low = tile > 0
    has_high = tile < tile_count - 1
    near = [
        (has_front, me - 1, tile),
        (has_behind, me + 1, tile),
        (has_low, me, tile - 1),
        (has_high, me, tile + 1),
        (has_front & has_low, me - 1, tile - 1),
        (has_front & has_high, me - 1, tile + 1),
        (has_behind & has_low, me + 1, tile - 1),
        (has_behind & has_high, me + 1, tile + 1),
    ]
    barrier = pltpu.get_barrier_semaphore()
    for cond, d, t in near:
        @pl.when(cond)
        def _(d=d, t=t):
            pl.semaphore_signal(barrier, inc=1, device_id=(d, t), device_id_type=pl.DeviceIdType.MESH)
    pl.semaphore_signal(barrier, inc=1, device_id=(partner, tile), device_id_type=pl.DeviceIdType.MESH)
    for step in range(chips - 1):
        other = (chip + step + 1) % chips * 2 + core
        pl.semaphore_signal(barrier, inc=1, device_id=(other, tile), device_id_type=pl.DeviceIdType.MESH)
    def spread(source, p):
        for r in range(0, rows, SUB):
            for j in range(cols // LANE):
                grid[p, pl.ds((r + 1) * SUB + j, SUB, stride=SUB), :] = source[
                    r : r + SUB, j * LANE : (j + 1) * LANE
                ]

    first, last = pl.ds(SUB, SUB), pl.ds(rows * SUB, SUB)
    def settle(p):
        loads[p].wait()
        spread(raw.at[p], p)
        low_send[p] = grid[p, first, :]
        high_send[p] = grid[p, last, :]

    settle(0)
    greeted = chips
    for cond, _, _ in near:
        greeted = greeted + cond.astype(jnp.int32)
    pl.semaphore_wait(barrier, greeted)

    block = 2 * share
    sends = []

    def plane_row(row, count):
        return grid.at[0, pl.ds(pl.multiple_of((row + 1) * SUB, SUB), count * SUB), :]

    def turn(at, step):
        return (at + (2 * (at % 2) - 1) * (step + 1) + chips) % chips

    strips = []
    for step in range(chips):
        q = turn((me + depth_count - 1) // 2 % chips, step)
        strip = []
        for k, (cond, row, count, place) in enumerate((
            (has_front, q * block, block, 1),
            (has_front & (q > 0), jnp.maximum(q * block - 1, 0), 1, 0),
            (has_front & (q < chips - 1), jnp.minimum((q + 1) * block, rows - 1), 1, block + 1),
        )):
            copy = remote(
                plane_row(row, count), behind.at[step, pl.ds(place * SUB, count * SUB), :],
                plane_send_sem.at[step, k], plane_recv_sem.at[step, k], me - 1, tile,
            )
            sends.append((cond, copy))
            strip.append(copy)
        strips.append(strip)

    def launch(copies):
        for cond, copy in copies:
            @pl.when(cond)
            def _(copy=copy):
                copy.start()

    launch(sends)
    for p in range(1, planes):
        settle(p)
    own = pl.ds(0, planes)
    to_low = remote(low_send, high.at[own], edge_send_sem.at[0], edge_recv_sem.at[0], me, tile - 1)
    to_high = remote(high_send, low.at[own], edge_send_sem.at[1], edge_recv_sem.at[1], me, tile + 1)
    corner_low = remote(
        low_send.at[0], high.at[planes], edge_send_sem.at[2], edge_recv_sem.at[2], me - 1, tile - 1
    )
    corner_high = remote(
        high_send.at[0], low.at[planes], edge_send_sem.at[3], edge_recv_sem.at[3], me - 1, tile + 1
    )
    edges = [
        (has_low, to_low),
        (has_high, to_high),
        (has_front & has_low, corner_low),
        (has_front & has_high, corner_high),
    ]
    launch(edges)

    below, above = pl.ds(0, SUB), pl.ds((rows + 1) * SUB, SUB)
    blank = jnp.zeros((SUB, LANE), jnp.float32)

    def fill(cond, copy, where, halo, which):
        @pl.when(cond)
        def _():
            copy.wait_recv()
            for p in which:
                grid[p, where, :] = halo[p]

        @pl.when(jnp.logical_not(cond))
        def _():
            for p in which:
                grid[p, where, :] = blank

    lane = lax.broadcasted_iota(jnp.int32, (group, SUB, LANE), 2)
    sub = lax.broadcasted_iota(jnp.int32, (group, SUB, LANE), 1)
    left_edge = lane == 0
    right_edge = lane == LANE - 1
    left_end = left_edge & (sub == 0)
    right_end = right_edge & (sub == SUB - 1)
    scale = spacing * LOG2E

    def plane_step(p, row, state, there):
        red, blue, green, through = state
        at = pl.ds(pl.multiple_of(row * SUB, SUB), (group + 2) * SUB)
        here = grid[p, at, :].reshape(group + 2, SUB, LANE)
        there = there.reshape(group + 2, SUB, LANE)
        total = here + there
        twice = total[1:-1]
        d_depth = there[1:-1] - here[1:-1]
        d_rows = total[2:] - total[:-2]
        from_left = pltpu.roll(twice, 1, 2)
        from_left = jnp.where(left_edge, pltpu.roll(from_left, 1, 1), from_left)
        from_left = jnp.where(left_end, 0.0, from_left)
        from_right = pltpu.roll(twice, LANE - 1, 2)
        from_right = jnp.where(right_edge, pltpu.roll(from_right, SUB - 1, 1), from_right)
        from_right = jnp.where(right_end, 0.0, from_right)
        d_cols = from_right - from_left
        facing = (0.25 * light_cols) * d_cols + (0.25 * light_rows) * d_rows + light_depth * d_depth
        length = (d_cols * d_cols + d_rows * d_rows) * 0.0625 + (d_depth * d_depth + 1.0)
        shading = 0.3 + 0.7 * jnp.abs(facing) * lax.rsqrt(length)
        optics = scale * floor_density
        for centre, width, bump in zip(centres, spreads, heights):
            root = math.sqrt(LOG2E) / width
            scaled = (0.5 * root) * twice - root * centre
            optics = optics + jnp.exp2(math.log2(bump * scale) - scaled * scaled)
        after = through * jnp.exp2(-optics)
        lit = (through - after) * shading
        middle = jnp.exp2((twice * (-0.25 * LOG2E)) * twice)
        balance = jnp.tanh(0.5 * twice)
        return (red + lit, blue + lit * balance, green + lit * middle, after)

    width = share * SUB

    def put(chunk, offset, state):
        at = pl.ds(pl.multiple_of(offset * SUB, SUB), group * SUB)
        for c in range(4):
            parts[chunk, c, at, :] = state[c].reshape(group * SUB, LANE)

    zero = jnp.zeros((group, SUB, LANE), jnp.float32)
    per_share = share // group

    def window(row):
        return pl.ds(pl.multiple_of(row * SUB, SUB), (group + 2) * SUB)

    order = [turn(chip, step) for step in range(chips)]

    def early(i, carry):
        state = (zero, zero, zero, zero + 1.0)
        for p in range(planes - 1):
            state = plane_step(p, i * group, state, grid[p + 1, window(i * group), :])
        put(i // per_share, i % per_share * group, state)
        return carry

    def end(step, cond, have, copy, halo, place):
        at = pl.ds(place * SUB, SUB)

        @pl.when(cond & have)
        def _():
            copy.wait_recv()
            behind[step, at, :] = halo[planes]

        @pl.when(cond & jnp.logical_not(have))
        def _():
            behind[step, at, :] = blank

    def arrive(step):
        q = order[step]
        whole, lower, upper = strips[step]

        @pl.when(has_behind)
        def _():
            whole.wait_recv()

        @pl.when(has_behind & (q > 0))
        def _():
            lower.wait_recv()

        @pl.when(has_behind & (q < chips - 1))
        def _():
            upper.wait_recv()

        end(step, has_behind & (q == 0), has_low, corner_high, low, 0)
        end(step, has_behind & (q == chips - 1), has_high, corner_low, high, block + 1)

        @pl.when(jnp.logical_not(has_behind))
        def _():
            behind[step] = jnp.zeros(behind.shape[1:], jnp.float32)

    def late(step, side):
        chunk = order[step] * 2 + side

        def body(i, carry):
            at = pl.ds(pl.multiple_of(i * group * SUB, SUB), group * SUB)
            state = tuple(parts[chunk, c, at, :].reshape(group, SUB, LANE) for c in range(4))
            there = behind[step, window(side * share + i * group), :]
            put(chunk, i * group, plane_step(planes - 1, chunk * share + i * group, state, there))
            return carry

        lax.fori_loop(0, per_share, body, 0)

    groups = rows // group
    lax.fori_loop(1, groups - 1, early, 0)
    fill(has_high, to_low, above, high, range(planes))
    fill(has_low, to_high, below, low, range(planes))
    lax.fori_loop(0, 2, lambda i, carry: early(i * (groups - 1), carry), 0)

    in_front = core == 0
    pair_copies = []
    piece_copies = []

    def combine(step):
        q = order[step]
        pair_copies[step].wait_recv()
        chunk = q * 2 + core
        mine = [parts[chunk, c] for c in range(4)]
        theirs = [pair[step, c] for c in range(4)]
        near_through = jnp.where(in_front, mine[3], theirs[3])
        final = step == chips - 1
        target = pieces.at[chip] if final else send.at[step]
        for c in range(3):
            target[c] = jnp.where(in_front, mine[c], theirs[c]) + near_through * jnp.where(in_front, theirs[c], mine[c])
        target[3] = mine[3] * theirs[3]
        if not final:
            copy = remote(
                send.at[step], pieces.at[chip], piece_send_sem.at[step], piece_recv_sem.at[step],
                q * 2 + core, tile,
            )
            copy.start()
            piece_copies.append(copy)

    for step, q in enumerate(order):
        arrive(step)
        late(step, 1 - core)
        copy = remote(
            parts.at[q * 2 + (1 - core)], pair.at[step], pair_send_sem.at[step], pair_recv_sem.at[step], partner, tile
        )
        copy.start()
        pair_copies.append(copy)
        late(step, core)
        if step > 0:
            combine(step - 1)
    combine(chips - 1)

    for copy in piece_copies:
        copy.wait_recv()
    colour = [pieces[0, c] for c in range(3)]
    through = pieces[0, 3]
    for k in range(1, chips):
        colour = [colour[c] + through * pieces[k, c] for c in range(3)]
        through = through * pieces[k, 3]
    image = (0.5 * (colour[0] + colour[1]), colour[2], 0.5 * (colour[0] - colour[1]), through)
    for c in range(4):
        result[:, c * SUB : (c + 1) * SUB, :] = image[c].reshape(share, SUB, LANE)
    for j in range(cols // LANE):
        out[:, :, j * LANE : (j + 1) * LANE] = result[:, pl.ds(j, 4, stride=SUB), :]

    for copy in pair_copies + piece_copies:
        copy.wait_send()
    for cond, copy in edges + sends:
        @pl.when(cond)
        def _(copy=copy):
            copy.wait_send()


def local(field):
    planes, rows, cols = field.shape
    depth_count = lax.axis_size("depth")
    chips = depth_count // 2
    share = rows // depth_count
    f32 = jnp.float32
    dims = (planes, rows, cols, depth_count, lax.axis_size("tile"))
    dma = pltpu.SemaphoreType.DMA
    image = pl.pallas_call(
        functools.partial(kernel, dims),
        out_shape=jax.ShapeDtypeStruct((share, 4, cols), f32),
        in_specs=[pl.BlockSpec(memory_space=pltpu.HBM)],
        out_specs=pl.BlockSpec(memory_space=pltpu.VMEM),
        scratch_shapes=[
            pltpu.VMEM((planes, rows, cols), f32),
            pltpu.VMEM((chips, (2 * share + 2) * SUB, LANE), f32),
            pltpu.VMEM((planes, (rows + 2) * SUB, LANE), f32),
            pltpu.VMEM((planes, SUB, LANE), f32),
            pltpu.VMEM((planes, SUB, LANE), f32),
            pltpu.VMEM((planes + 1, SUB, LANE), f32),
            pltpu.VMEM((planes + 1, SUB, LANE), f32),
            pltpu.VMEM((depth_count, 4, share * SUB, LANE), f32),
            pltpu.VMEM((chips, 4, share * SUB, LANE), f32),
            pltpu.VMEM((chips, 4, share * SUB, LANE), f32),
            pltpu.VMEM((chips, 4, share * SUB, LANE), f32),
            pltpu.VMEM((share, 4 * SUB, LANE), f32),
            dma((planes,)),
            dma((chips, 3)),
            dma((chips, 3)),
            dma((4,)),
            dma((4,)),
            dma((chips,)),
            dma((chips,)),
            dma((chips,)),
            dma((chips,)),
        ],
        compiler_params=pltpu.CompilerParams(
            collective_id=0, has_side_effects=True, vmem_limit_bytes=55_000_000
        ),
    )(field)
    image = jnp.transpose(image, (1, 0, 2))
    channel = lax.broadcasted_iota(jnp.int32, image.shape, 0)
    return jnp.where(channel == 3, 1.0 - image, image)


def solution(mesh):
    return jax.shard_map(
        local,
        mesh=mesh,
        in_specs=(P("depth", "tile", None),),
        out_specs=P(None, ("tile", "depth"), None),
        check_vma=False,
    )
```
